32 devices in a mesh: groups: 2 (over x), epoch: 4 (over y, core), param: 4 (over z).
Axes of the slice: x: 2, y: 2, z: 4, core: 2. Of those that a mesh axis runs over, the one named last changes fastest.
Arguments:
- probes: bfloat16 [128, 65536], P(('groups', 'epoch'), 'param'), parts along dimension 0, may hold values from -0.0234375 to 0.0234375
- lat_bin: int32 [4096], P('epoch'), may hold values from 0 to 254
- lat_frac: float32 [4096], P('epoch'), may hold values from 0 to 1
- longitude: float32 [4096], P('epoch'), may hold values from -3.140625 to 3.140625
- order_code: int32 [65536], P('param'), may hold values from 0 to 511
- legendre: bfloat16 [256, 65536], P(None, 'param'), may hold values from -6 to 6
- bank: float32 [8, 255], replicated, may hold values from -0.01171875 to 0.01171875
- seg_filter: int32 [16], P('epoch'), may hold values from 0 to 7
Outputs:
- residual: float32 [128, 65536], P(('groups', 'epoch'), 'param'), parts along dimension 0
The draws below stay inside these ranges and needn't reach their ends.
There are 2 independent parts, one for each index of `groups`. The reference program is written for one: setup_inputs(seed, part) draws one part's arguments, and reference() takes and returns one part's arrays. A program takes and returns all parts, laid end to end along the dimension named above; an argument that names none is the same for every part. Nothing has to cross between parts.
All inputs are finite; a program needn't handle non-finite values.
Results may differ from the reference program's by a relative error of at most 0.0061.
Values may be sent and summed in bfloat16 or wider, within the bound.
No kernel may reach another device: no remote copies, remote signals or barrier semaphores. Data moves between devices by JAX's collectives and lax.ppermute only.
A program may use at most 192 MiB of HBM per device.

```python
import jax
import jax.numpy as jnp
from jax import lax

COEFFS = 65536
ORDERS = 256
KBINS = 256
PROBES = 64
TAPS = 255
NFILT = 8
SEG = 256
TILE = 256
EPOCHS = 4096
NSEG = 16


def plant(array, stream_key, low, top_value):
    longest = array.shape.index(max(array.shape))
    spots = []
    for shift in (0, 1):
        where = [jax.random.randint(jax.random.fold_in(stream_key, axis), (), 0, length) for axis, length in enumerate(array.shape)]
        where[longest] = (where[longest] + shift) % array.shape[longest]
        spots.append(tuple(where))
    return array.at[spots[0]].set(low).at[spots[1]].set(top_value)


def levels(rng, dims, pieces, low, largest):
    loudness = 1.0
    for dim, parts in pieces:
        heights = jax.random.uniform(jax.random.fold_in(jax.random.fold_in(rng, 6), dim), (parts,), jnp.float32, low / len(pieces), largest / len(pieces))
        loudness = loudness * jnp.repeat(jnp.exp(heights), dims[dim] // parts).reshape((-1,) + (1,) * (len(dims) - 1 - dim))
    return loudness


def gaussian(key, shape, spread, most, shards=(), kind=jnp.bfloat16):
    entries = spread * jax.random.normal(key, shape, jnp.float32)
    if shards:
        entries = entries * levels(key, shape, shards, -0.22, 0.18)
    return jnp.clip(entries, -most, most).astype(kind)


def setup_inputs(seed: int = 0, part: int = 0) -> dict:
    key_list = jax.random.split(jax.random.key(seed), 9)
    part_splits = jax.random.split(jax.random.fold_in(key_list[8], part), 9)
    return {
        "probes": gaussian(part_splits[0], (PROBES, COEFFS), COEFFS ** -0.5, 0.0234375, ((0, 4), (1, 4))),
        "lat_bin": plant(jax.random.randint(key_list[1], (EPOCHS,), 0, KBINS - 1), jax.random.fold_in(key_list[1], 1), 0, (KBINS - 1) - 1).astype(jnp.int32),
        "lat_frac": jnp.clip(1.0 * jax.random.uniform(key_list[2], (EPOCHS,), jnp.float32) ** levels(key_list[2], (EPOCHS,), ((0, 4),), -0.2, 0.2), 0.0, 1.0),
        "longitude": jnp.clip(jax.random.uniform(key_list[3], (EPOCHS,), jnp.float32, -3.140625, 3.140625), -3.140625, 3.140625),
        "order_code": plant(jax.random.randint(key_list[4], (COEFFS,), 0, 2 * ORDERS), jax.random.fold_in(key_list[4], 1), 0, (2 * ORDERS) - 1).astype(jnp.int32),
        "legendre": gaussian(key_list[5], (KBINS, COEFFS), 1.0, 6.0, ((1, 4),)),
        "bank": gaussian(key_list[6], (NFILT, TAPS), (TAPS * EPOCHS // 4) ** -0.5, 0.01171875, (), jnp.float32),
        "seg_filter": plant(jax.random.randint(key_list[7], (NSEG,), 0, NFILT), jax.random.fold_in(key_list[7], 1), 0, NFILT - 1).astype(jnp.int32),
    }


HALF_PI = 1.5707963267948966


def design_rows(bins, fraction, angles, legendre, order_code):
    lower_weight = lax.optimization_barrier((1.0 - fraction).astype(jnp.bfloat16)).astype(jnp.float32)
    upper_weight = lax.optimization_barrier(fraction.astype(jnp.bfloat16)).astype(jnp.float32)
    table_rows = legendre.astype(jnp.float32)
    interp = lower_weight[:, None] * table_rows[bins] + upper_weight[:, None] * table_rows[bins + 1]
    orders = (order_code // 2).astype(jnp.float32)
    is_sine = (order_code % 2).astype(jnp.float32)
    phases = jnp.cos(angles[:, None] * orders[None, :] - is_sine[None, :] * HALF_PI)
    return (interp * phases).astype(jnp.bfloat16)


def reference(probes, lat_bin, lat_frac, longitude, order_code, legendre, bank, seg_filter):
    tile_count = EPOCHS // TILE
    bins_tiled = lat_bin.reshape(tile_count, TILE)
    frac_tiled = lat_frac.reshape(tile_count, TILE)
    angle_tiled = longitude.reshape(tile_count, TILE)
    probe_float = probes.astype(jnp.float32)

    def forward(piece_item):
        design = design_rows(piece_item[0], piece_item[1], piece_item[2], legendre, order_code).astype(jnp.float32)
        return jnp.dot(probe_float, design.T, precision=lax.Precision.HIGHEST)

    prediction = lax.map(forward, (bins_tiled, frac_tiled, angle_tiled))
    prediction = jnp.transpose(prediction, (1, 0, 2)).reshape(PROBES, EPOCHS)
    segment_of = jnp.arange(EPOCHS, dtype=jnp.int32) // SEG
    taps_of = bank[seg_filter[segment_of]]
    padded = jnp.pad(prediction, ((0, 0), (TAPS - 1, 0)))

    def add_tap(lag_index, total_sum):
        offset = (TAPS - 1 - lag_index).astype(jnp.int32)
        window = lax.dynamic_slice(padded, (jnp.int32(0), offset), (PROBES, EPOCHS))
        column = lax.dynamic_slice_in_dim(taps_of, lag_index.astype(jnp.int32), 1, 1)[:, 0]
        return total_sum + column[None, :] * window

    filtered = lax.fori_loop(jnp.int32(0), jnp.int32(TAPS), add_tap, jnp.zeros((PROBES, EPOCHS), jnp.float32))
    filtered = lax.optimization_barrier(filtered.astype(jnp.bfloat16)).astype(jnp.float32)
    filtered_tiled = jnp.transpose(filtered.reshape(PROBES, tile_count, TILE), (1, 0, 2))

    def backward(total_sum, piece_item):
        design = design_rows(piece_item[1], piece_item[2], piece_item[3], legendre, order_code).astype(jnp.float32)
        return total_sum + jnp.dot(piece_item[0], design, precision=lax.Precision.HIGHEST), None

    residual, unused = lax.scan(backward, jnp.zeros((PROBES, COEFFS), jnp.float32), (filtered_tiled, bins_tiled, frac_tiled, angle_tiled))
    return residual
```

```python
import functools

import jax
import jax.numpy as jnp
from jax import lax
from jax.experimental import pallas as pl
from jax.experimental.pallas import tpu as pltpu
from jax.sharding import PartitionSpec as P

SEG = 256
ORDERS = 256
ROWS = 256
COLS = 1024
INV_TWO_PI = 0.15915494309189535
TWO_PI_HI = 6.28125
TWO_PI_LO = 0.0019353071795864769
COS = (1.0, -1 / 2, 1 / 24, -1 / 720, 1 / 40320, -1 / 3628800, 1 / 479001600, -1 / 87178291200, 1 / 20922789888000)
SIN = (1.0, -1 / 6, 1 / 120, -1 / 5040, 1 / 362880, -1 / 39916800, 1 / 6227020800, -1 / 1307674368000, 1 / 355687428096000)
BF16 = jnp.bfloat16
F32 = jnp.float32


def horner(coefficients, x):
    total = coefficients[-1]
    for coefficient in coefficients[-2::-1]:
        total = total * x + coefficient
    return total


def dot(a, b):
    return jnp.dot(a, b, preferred_element_type=F32)


def dot_t(a, b):
    return lax.dot_general(a, b, (((1,), (1,)), ((), ())), preferred_element_type=F32)


def column(row_ref):
    row = row_ref[...].astype(F32)
    return jnp.transpose(jnp.broadcast_to(row, (8, row.shape[1])))[:, :1]


def fill_tables(bin_ref, frac_ref, lon_ref, weights_ref, trig_ref):
    nodes = weights_ref.shape[1]
    bins, fraction, angles = column(bin_ref), column(frac_ref), column(lon_ref)
    node = lax.broadcasted_iota(jnp.int32, (1, nodes), 1).astype(F32)
    order = lax.broadcasted_iota(jnp.int32, (1, ORDERS), 1).astype(F32)
    for first in range(0, weights_ref.shape[0], ROWS):
        rows = slice(first, first + ROWS)
        b, f = bins[rows], fraction[rows]
        lower = jnp.where(node == b, 1.0 - f, 0.0)
        upper = jnp.where(node == b + 1.0, f, 0.0)
        weights_ref[rows, :] = (lower + upper).astype(BF16)
        angle = angles[rows] * order
        turns = jnp.round(angle * INV_TWO_PI)
        rest = (angle - turns * TWO_PI_HI) - turns * TWO_PI_LO
        square = rest * rest
        trig_ref[rows, :ORDERS] = horner(COS, square).astype(BF16)
        trig_ref[rows, ORDERS:] = (rest * horner(SIN, square)).astype(BF16)


def design_tile(weights_ref, trig_ref, code_ref, legendre_ref, rows, chosen):
    interp = dot(weights_ref[rows, :], legendre_ref[...])
    phases = dot(trig_ref[rows, :], chosen)
    return (interp * phases).astype(BF16)


def one_hot(code_ref):
    code = code_ref[...]
    place = lax.shift_right_logical(code, 1) + (code & 1) * ORDERS
    index = lax.broadcasted_iota(jnp.int32, (2 * ORDERS, 1), 0)
    return jnp.where(index == place, 1.0, 0.0).astype(BF16)


def first_kernel(bin_ref, frac_ref, lon_ref, code_ref, legendre_ref, design_ref, weights_ref, trig_ref):
    @pl.when(pl.program_id(0) == 0)
    def _():
        fill_tables(bin_ref, frac_ref, lon_ref, weights_ref, trig_ref)

    chosen = one_hot(code_ref)
    for first in range(0, design_ref.shape[0], ROWS):
        rows = slice(first, first + ROWS)
        design_ref[rows, :] = design_tile(weights_ref, trig_ref, code_ref, legendre_ref, rows, chosen)


def second_kernel(weights_ref, trig_ref, code_ref, legendre_ref, probes_ref, old_ref, old_probes_ref,
                  design_ref, pred_ref, sent_ref, total_ref):
    step = pl.program_id(0)

    @pl.when(step == 0)
    def _():
        total_ref[...] = jnp.zeros_like(total_ref)

    chosen = one_hot(code_ref)
    for first in range(0, design_ref.shape[0], ROWS):
        rows = slice(first, first + ROWS)
        tile = design_tile(weights_ref, trig_ref, code_ref, legendre_ref, rows, chosen)
        design_ref[rows, :] = tile
        total_ref[rows, :] += dot_t(tile, probes_ref[...]) + dot_t(old_ref[rows, :], old_probes_ref[...])

    @pl.when(step == pl.num_programs(0) - 1)
    def _():
        total = jnp.transpose(total_ref[...])
        pred_ref[...] = total
        sent_ref[...] = total.astype(BF16)


def filter_kernel(seg_ref, bank_ref, before_ref, pred_ref, out_ref):
    for segment in range(pred_ref.shape[1] // SEG):
        taps = bank_ref[pl.ds(seg_ref[segment], 1), :]
        spread = jnp.broadcast_to(taps, (2 * SEG, 2 * SEG))
        table = pltpu.roll(spread, SEG, 1, stride=1, stride_axis=0)[:, :SEG]
        here = pred_ref[:, segment * SEG : (segment + 1) * SEG]
        past = before_ref[...] if segment == 0 else pred_ref[:, (segment - 1) * SEG : segment * SEG]
        window = jnp.concatenate([past, here], axis=1)
        value = jnp.dot(window, table, precision=lax.Precision.HIGHEST, preferred_element_type=F32)
        out_ref[:, segment * SEG : (segment + 1) * SEG] = value.astype(BF16)


def residual_kernel(filtered_ref, design_ref, kept_ref, sent_ref):
    value = dot(filtered_ref[...], design_ref[...])
    half = kept_ref.shape[0]
    kept_ref[...] = value[:half]
    sent_ref[...] = value[half:].astype(BF16)


def struct(shape, dtype):
    return jax.ShapeDtypeStruct(shape, dtype)


def whole(shape):
    return pl.BlockSpec(shape, lambda c: (0,) * len(shape))


def across(rows, cols, shift=0):
    return pl.BlockSpec((rows, cols), lambda c: (0, c + shift))


def cost(flops, nbytes):
    return pl.CostEstimate(flops=flops, bytes_accessed=nbytes, transcendentals=0)


def swapped(array, axis, bit):
    size = lax.axis_size(axis)
    return lax.ppermute(array, axis, [(i, i ^ bit) for i in range(size)])


def bits_of(axis):
    return [1 << b for b in range(lax.axis_size(axis).bit_length() - 1)]


def local(probes, lat_bin, lat_frac, longitude, order_code, legendre, bank, seg_filter):
    epochs, (nodes, coeffs) = lat_bin.shape[0], legendre.shape
    own = probes.shape[0]
    epoch_bits = bits_of("epoch")
    row = lambda array: array.reshape(1, -1)
    codes = row(order_code)
    half = coeffs // 2
    cols = min(COLS, half)
    steps = half // cols

    gathered = probes
    for bit in reversed(epoch_bits):
        gathered = jnp.concatenate([gathered, swapped(gathered, "epoch", bit)], axis=0)
    count = gathered.shape[0]

    design_1, weights, trig = pl.pallas_call(
        first_kernel,
        grid=(steps,),
        in_specs=[whole((1, epochs))] * 3 + [across(1, cols), across(nodes, cols)],
        out_specs=[across(epochs, cols), whole((epochs, nodes)), whole((epochs, 2 * ORDERS))],
        out_shape=[struct((epochs, half), BF16), struct((epochs, nodes), BF16), struct((epochs, 2 * ORDERS), BF16)],
        cost_estimate=cost(2 * epochs * half * (nodes + 2 * ORDERS), 2 * half * (epochs + nodes)),
        name="design_first",
    )(row(lat_bin), row(lat_frac), row(longitude), codes, legendre)

    design_2, pred, sent = pl.pallas_call(
        second_kernel,
        grid=(steps,),
        in_specs=[
            whole((epochs, nodes)),
            whole((epochs, 2 * ORDERS)),
            across(1, cols, steps),
            across(nodes, cols, steps),
            across(count, cols, steps),
            across(epochs, cols),
            across(count, cols),
        ],
        out_specs=[across(epochs, cols), whole((count, epochs)), whole((count, epochs))],
        out_shape=[struct((epochs, half), BF16), struct((count, epochs), F32), struct((count, epochs), BF16)],
        scratch_shapes=[pltpu.VMEM((epochs, count), F32)],
        cost_estimate=cost(2 * epochs * half * (nodes + 2 * ORDERS + 2 * count), 2 * half * (2 * epochs + nodes)),
        name="design_second",
    )(weights, trig, codes, legendre, gathered, design_1, gathered)

    for bit in bits_of("param"):
        pred = pred + swapped(sent, "param", bit).astype(F32)
        sent = pred.astype(BF16)

    devices = lax.axis_size("epoch")
    before = lax.ppermute(pred[:, epochs - SEG :], "epoch", [(i, i + 1) for i in range(devices - 1)])
    here = lax.axis_index("epoch")
    differing = here ^ (here - 1)
    before = before.reshape((2,) * len(epoch_bits) + (own, SEG))
    for place, bit in enumerate(epoch_bits):
        before = jnp.where((differing & bit) != 0, jnp.flip(before, place), before)
    before = before.reshape(count, SEG)

    taps = jnp.pad(bank, ((0, 0), (0, 2 * SEG - bank.shape[1])))
    filtered = pl.pallas_call(
        filter_kernel,
        in_specs=[pl.BlockSpec(memory_space=pltpu.SMEM)] + [pl.BlockSpec(memory_space=pltpu.VMEM)] * 3,
        out_specs=pl.BlockSpec(memory_space=pltpu.VMEM),
        out_shape=struct((count, epochs), BF16),
        cost_estimate=cost(12 * count * epochs * 2 * SEG, 8 * count * epochs),
        name="filter",
    )(seg_filter, taps, before, pred)

    pieces = []
    for design in (design_1, design_2):
        kept, sent = pl.pallas_call(
            residual_kernel,
            grid=(steps,),
            in_specs=[whole((count, epochs)), across(epochs, cols)],
            out_specs=[across(count // 2, cols)] * 2,
            out_shape=[struct((count // 2, half), F32), struct((count // 2, half), BF16)],
            cost_estimate=cost(2 * count * epochs * half, 2 * epochs * half),
            name="residual",
        )(filtered, design)
        for bit in epoch_bits[:-1]:
            total = kept + swapped(sent, "epoch", bit).astype(F32)
            rows = total.shape[0] // 2
            kept, sent = total[:rows], total[rows:].astype(BF16)
        pieces.append(kept + swapped(sent, "epoch", epoch_bits[-1]).astype(F32))
    return jnp.concatenate(pieces, axis=1)


def solution(mesh):
    placed = (
        P(("groups", "epoch"), "param"),
        P("epoch"),
        P("epoch"),
        P("epoch"),
        P("param"),
        P(None, "param"),
        P(),
        P("epoch"),
    )
    return jax.shard_map(
        local,
        mesh=mesh,
        in_specs=placed,
        out_specs=P(("groups", "epoch"), "param"),
        check_vma=False,
    )
```

```python
import functools

import jax
import jax.numpy as jnp
from jax import lax
from jax.experimental import pallas as pl
from jax.experimental.pallas import tpu as pltpu
from jax.sharding import PartitionSpec as P


SEG = 256
ORDERS = 256
ROWS = 256
COLS = 1024
KERNEL_VMEM = 10 << 20
SMALL_VMEM = 6 << 20
INV_TWO_PI = 0.15915494309189535
TWO_PI_HI = 6.28125
TWO_PI_LO = 0.0019353071795864769
COS = (1.0, -1 / 2, 1 / 24, -1 / 720, 1 / 40320, -1 / 3628800, 1 / 479001600, -1 / 87178291200, 1 / 20922789888000)
SIN = (1.0, -1 / 6, 1 / 120, -1 / 5040, 1 / 362880, -1 / 39916800, 1 / 6227020800, -1 / 1307674368000, 1 / 355687428096000)
BF16 = jnp.bfloat16
F32 = jnp.float32


def horner(coefficients, x):
    total = coefficients[-1]
    for coefficient in coefficients[-2::-1]:
        total = total * x + coefficient
    return total


def dot(a, b):
    return jnp.dot(a, b, preferred_element_type=F32)


def dot_t(a, b):
    return lax.dot_general(a, b, (((1,), (1,)), ((), ())), preferred_element_type=F32)


def column(row_ref):
    row = row_ref[...].astype(F32)
    return jnp.transpose(jnp.broadcast_to(row, (8, row.shape[1])))[:, :1]


def fill_tables(bin_ref, frac_ref, lon_ref, weights_ref, trig_ref):
    nodes = weights_ref.shape[1]
    bins, fraction, angles = column(bin_ref), column(frac_ref), column(lon_ref)
    node = lax.broadcasted_iota(jnp.int32, (1, nodes), 1).astype(F32)
    order = lax.broadcasted_iota(jnp.int32, (1, ORDERS), 1).astype(F32)
    for first in range(0, weights_ref.shape[0], ROWS):
        rows = slice(first, first + ROWS)
        b, f = bins[rows], fraction[rows]
        lower = jnp.where(node == b, 1.0 - f, 0.0)
        upper = jnp.where(node == b + 1.0, f, 0.0)
        weights_ref[rows, :] = (lower + upper).astype(BF16)
        angle = angles[rows] * order
        turns = jnp.round(angle * INV_TWO_PI)
        rest = (angle - turns * TWO_PI_HI) - turns * TWO_PI_LO
        square = rest * rest
        trig_ref[rows, :ORDERS] = horner(COS, square).astype(BF16)
        trig_ref[rows, ORDERS:] = (rest * horner(SIN, square)).astype(BF16)


def design_tile(weights_ref, trig_ref, legendre_ref, rows, chosen):
    interp = dot(weights_ref[rows, :], legendre_ref[...])
    phases = dot(trig_ref[rows, :], chosen)
    return (interp * phases).astype(BF16)


def one_hot(code_ref):
    code = code_ref[...]
    place = lax.shift_right_logical(code, 1) + (code & 1) * ORDERS
    index = lax.broadcasted_iota(jnp.int32, (2 * ORDERS, 1), 0)
    return jnp.where(index == place, 1.0, 0.0).astype(BF16)


def first_kernel(bin_ref, frac_ref, lon_ref, code_ref, legendre_ref, design_ref, weights_ref, trig_ref):
    @pl.when(pl.program_id(0) == 0)
    def _():
        fill_tables(bin_ref, frac_ref, lon_ref, weights_ref, trig_ref)

    step = pl.program_id(0)
    chosen = one_hot(code_ref)
    for first in range(0, design_ref.shape[1], ROWS):
        rows = slice(first, first + ROWS)
        design_ref[step, rows, :] = design_tile(weights_ref, trig_ref, legendre_ref, rows, chosen)


def second_kernel(blocks, weights_ref, trig_ref, code_ref, legendre_ref, old_ref, *refs):
    probe_refs, old_probe_refs = refs[:blocks], refs[blocks : 2 * blocks]
    design_ref, pred_ref, sent_ref, total_ref = refs[2 * blocks :]
    step = pl.program_id(0)

    @pl.when(step == 0)
    def _():
        total_ref[...] = jnp.zeros_like(total_ref)

    probes = jnp.concatenate([ref[...] for ref in probe_refs], axis=0)
    old_probes = jnp.concatenate([ref[...] for ref in old_probe_refs], axis=0)
    chosen = one_hot(code_ref)
    for first in range(0, design_ref.shape[1], ROWS):
        rows = slice(first, first + ROWS)
        tile = design_tile(weights_ref, trig_ref, legendre_ref, rows, chosen)
        design_ref[step, rows, :] = tile
        total_ref[rows, :] += dot_t(tile, probes) + dot_t(old_ref[step, rows, :], old_probes)

    @pl.when(step == pl.num_programs(0) - 1)
    def _():
        total = jnp.transpose(total_ref[...])
        pred_ref[...] = total
        sent_ref[...] = total.astype(BF16)


def tables_kernel(seg_ref, bank_ref, high_ref, low_ref):
    for segment in range(high_ref.shape[0]):
        taps = bank_ref[pl.ds(seg_ref[segment], 1), :]
        spread = jnp.broadcast_to(taps, (2 * SEG, 2 * SEG))
        table = pltpu.roll(spread, SEG, 1, stride=1, stride_axis=0)[:, :SEG]
        high = table.astype(BF16)
        high_ref[segment] = high
        low_ref[segment] = (table - high.astype(F32)).astype(BF16)


def filter_kernel(bits, before_ref, pred_ref, high_ref, low_ref, out_ref):
    before = before_ref[...]
    count = before.shape[0]
    here = lax.axis_index("epoch")
    differing = here ^ (here - 1)
    place = lax.broadcasted_iota(jnp.int32, before.shape, 0)
    stride = count
    for bit in bits:
        stride //= 2
        up, down = pltpu.roll(before, stride, 0), pltpu.roll(before, count - stride, 0)
        flipped = jnp.where((place & stride) != 0, up, down)
        before = jnp.where((differing & bit) != 0, flipped, before)

    for segment in range(pred_ref.shape[1] // SEG):
        here = pred_ref[:, segment * SEG : (segment + 1) * SEG]
        past = before if segment == 0 else pred_ref[:, (segment - 1) * SEG : segment * SEG]
        window = jnp.concatenate([past, here], axis=1)
        high = window.astype(BF16)
        low = (window - high.astype(F32)).astype(BF16)
        value = dot(high, high_ref[segment]) + (dot(high, low_ref[segment]) + dot(low, high_ref[segment]))
        out_ref[:, segment * SEG : (segment + 1) * SEG] = value.astype(BF16)


def residual_kernel(filtered_ref, design_ref, kept_ref, sent_ref):
    value = dot(filtered_ref[...], design_ref[pl.program_id(0)])
    half = kept_ref.shape[0]
    kept_ref[...] = value[:half]
    sent_ref[...] = value[half:].astype(BF16)


def struct(shape, dtype):
    return jax.ShapeDtypeStruct(shape, dtype)


def whole(shape):
    return pl.BlockSpec(shape, lambda c: (0,) * len(shape))


def across(rows, cols, shift=0):
    return pl.BlockSpec((rows, cols), lambda c: (0, c + shift))


def resident(array):
    return pltpu.with_memory_space_constraint(array, pltpu.VMEM)


def cost(flops, nbytes):
    return pl.CostEstimate(flops=flops, bytes_accessed=nbytes, transcendentals=0)


def swapped(array, axis, bit):
    size = lax.axis_size(axis)
    return lax.ppermute(array, axis, [(i, i ^ bit) for i in range(size)])


def bits_of(axis):
    return [1 << b for b in range(lax.axis_size(axis).bit_length() - 1)]


def local(probes, lat_bin, lat_frac, longitude, order_code, legendre, bank, seg_filter):
    epochs, (nodes, coeffs) = lat_bin.shape[0], legendre.shape
    own = probes.shape[0]
    epoch_bits = bits_of("epoch")
    row = lambda array: array.reshape(1, -1)
    codes = row(order_code)
    legendre = pltpu.with_memory_space_constraint(legendre, pltpu.HBM)
    half = coeffs // 2
    cols = min(COLS, half)
    steps = half // cols

    vmem, smem = pl.BlockSpec(memory_space=pltpu.VMEM), pl.BlockSpec(memory_space=pltpu.SMEM)
    taps = jnp.pad(bank, ((0, 0), (0, 2 * SEG - bank.shape[1])))
    segments = epochs // SEG
    high, low = pl.pallas_call(
        tables_kernel,
        in_specs=[smem, vmem],
        out_specs=[vmem] * 2,
        out_shape=[struct((segments, 2 * SEG, SEG), BF16)] * 2,
        cost_estimate=cost(40 * segments * SEG * SEG, 8 * segments * SEG * SEG),
        compiler_params=pltpu.CompilerParams(vmem_limit_bytes=SMALL_VMEM),
        name="tables",
    )(seg_filter, taps)

    blocks = [probes]
    for bit in reversed(epoch_bits[1:]):
        blocks += [swapped(block, "epoch", bit) for block in blocks]

    design_1, weights, trig = pl.pallas_call(
        first_kernel,
        grid=(steps,),
        in_specs=[whole((1, epochs))] * 3 + [across(1, cols), across(nodes, cols)],
        out_specs=[vmem, whole((epochs, nodes)), whole((epochs, 2 * ORDERS))],
        out_shape=[
            pltpu.VMEM((steps, epochs, cols), BF16),
            struct((epochs, nodes), BF16),
            struct((epochs, 2 * ORDERS), BF16),
        ],
        cost_estimate=cost(2 * epochs * half * (nodes + 2 * ORDERS), 2 * half * (epochs + nodes)),
        compiler_params=pltpu.CompilerParams(vmem_limit_bytes=KERNEL_VMEM),
        name="design_first",
    )(row(lat_bin), row(lat_frac), row(longitude), codes, legendre)
    blocks, design_1 = lax.optimization_barrier((blocks, design_1))
    blocks = blocks + [swapped(block, "epoch", epoch_bits[0]) for block in blocks]
    count = own * len(blocks)
    if own % 16:
        blocks = [jnp.concatenate(blocks, axis=0)]
    height = blocks[0].shape[0]

    design_2, pred, sent = pl.pallas_call(
        functools.partial(second_kernel, len(blocks)),
        grid=(steps,),
        in_specs=[
            whole((epochs, nodes)),
            whole((epochs, 2 * ORDERS)),
            across(1, cols, steps),
            across(nodes, cols, steps),
            vmem,
        ]
        + [across(height, cols, steps)] * len(blocks)
        + [across(height, cols)] * len(blocks),
        out_specs=[vmem, whole((count, epochs)), whole((count, epochs))],
        out_shape=[
            pltpu.VMEM((steps, epochs, cols), BF16),
            struct((count, epochs), F32),
            struct((count, epochs), BF16),
        ],
        scratch_shapes=[pltpu.VMEM((epochs, count), F32)],
        cost_estimate=cost(2 * epochs * half * (nodes + 2 * ORDERS + 2 * count), 2 * half * (2 * epochs + nodes)),
        compiler_params=pltpu.CompilerParams(vmem_limit_bytes=KERNEL_VMEM),
        name="design_second",
    )(weights, trig, codes, legendre, resident(design_1), *blocks, *blocks)

    for bit in bits_of("param"):
        pred = pred + swapped(sent, "param", bit).astype(F32)
        sent = pred.astype(BF16)

    devices = lax.axis_size("epoch")
    before = lax.ppermute(pred[:, epochs - SEG :], "epoch", [(i, i + 1) for i in range(devices - 1)])
    filtered = pl.pallas_call(
        functools.partial(filter_kernel, epoch_bits),
        in_specs=[vmem] * 4,
        out_specs=vmem,
        out_shape=struct((count, epochs), BF16),
        cost_estimate=cost(6 * count * epochs * 2 * SEG, 8 * count * epochs),
        compiler_params=pltpu.CompilerParams(vmem_limit_bytes=SMALL_VMEM),
        name="filter",
    )(before, pred, high, low)

    pieces = []
    for design in (design_1, design_2):
        kept, sent = pl.pallas_call(
            residual_kernel,
            grid=(steps,),
            in_specs=[whole((count, epochs)), vmem],
            out_specs=[across(count // 2, cols)] * 2,
            out_shape=[struct((count // 2, half), F32), struct((count // 2, half), BF16)],
            cost_estimate=cost(2 * count * epochs * half, 6 * count * half),
            compiler_params=pltpu.CompilerParams(vmem_limit_bytes=SMALL_VMEM),
            name="residual",
        )(filtered, resident(design))
        for bit in epoch_bits[:-1]:
            total = kept + swapped(sent, "epoch", bit).astype(F32)
            rows = total.shape[0] // 2
            kept, sent = total[:rows], total[rows:].astype(BF16)
        filtered, sent = lax.optimization_barrier((filtered, sent))
        received = swapped(sent, "epoch", epoch_bits[-1])
        pieces.append(kept + received.astype(F32))
    return jnp.concatenate(pieces, axis=1)


def solution(mesh):
    placed = (
        P(("groups", "epoch"), "param"),
        P("epoch"),
        P("epoch"),
        P("epoch"),
        P("param"),
        P(None, "param"),
        P(),
        P("epoch"),
    )
    return jax.shard_map(
        local,
        mesh=mesh,
        in_specs=placed,
        out_specs=P(("groups", "epoch"), "param"),
        check_vma=False,
    )
```

```python
import functools

import jax
import jax.numpy as jnp
from jax import lax
from jax.experimental import pallas as pl
from jax.experimental.pallas import tpu as pltpu
from jax.sharding import PartitionSpec as P


SEG = 256
ORDERS = 256
ROWS = 256
COLS = 1024
LANES = 128
KERNEL_VMEM = 10 << 20
SMALL_VMEM = 6 << 20
INV_TWO_PI = 0.15915494309189535
TURN = 12582912.0
COS = (0.9999992251396179, -19.738981246948242, 64.92865753173828, -85.27162170410156, 58.79049301147461, -21.07110595703125)
SIN = (6.283185005187988, -41.341590881347656, 81.59994506835938, -76.61447143554688, 41.3428840637207, -12.471243858337402)
BF16 = jnp.bfloat16
F32 = jnp.float32


def horner(coefficients, x):
    total = coefficients[-1]
    for coefficient in coefficients[-2::-1]:
        total = total * x + coefficient
    return total


def dot(a, b):
    return jnp.dot(a, b, preferred_element_type=F32)


def dot_t(a, b):
    return lax.dot_general(a, b, (((1,), (1,)), ((), ())), preferred_element_type=F32)


def spread(row):
    return jnp.transpose(jnp.broadcast_to(row, (LANES, row.shape[1])))


def fraction_of(turns):
    return turns - ((turns + TURN) - TURN)


def trig_kernel(bin_ref, frac_ref, lon_ref, weights_ref, trig_ref):
    nodes = weights_ref.shape[1]
    lane = lax.broadcasted_iota(jnp.int32, (1, LANES), 1).astype(F32)
    for first in range(0, weights_ref.shape[0], LANES):
        rows = slice(first, first + LANES)
        bins, fraction = spread(bin_ref[:, rows].astype(F32)), spread(frac_ref[:, rows])
        lower, upper = 1.0 - fraction, fraction
        for at in range(0, nodes, LANES):
            distance = bins - (lane + at)
            value = jnp.where(distance == 0.0, lower, jnp.where(distance == -1.0, upper, 0.0))
            weights_ref[rows, at : at + LANES] = value.astype(BF16)
        turns_row = lon_ref[:, rows] * INV_TWO_PI
        turns = spread(turns_row)
        rest, far = fraction_of(turns * lane), fraction_of(turns_row * LANES)
        square, far_square = rest * rest, far * far
        cos, sin = horner(COS, square), rest * horner(SIN, square)
        far_cos, far_sin = spread(horner(COS, far_square)), spread(far * horner(SIN, far_square))
        for part in range(ORDERS // LANES):
            if part:
                cos, sin = cos * far_cos - sin * far_sin, sin * far_cos + cos * far_sin
            at = part * LANES
            trig_ref[rows, at : at + LANES] = cos.astype(BF16)
            trig_ref[rows, ORDERS + at : ORDERS + at + LANES] = sin.astype(BF16)


def one_hot(code):
    place = lax.shift_right_logical(code, 1) + (code & 1) * ORDERS
    index = lax.broadcasted_iota(jnp.int32, (2 * ORDERS, 1), 0)
    return jnp.where(index == place, 1.0, 0.0).astype(BF16)


def design_tile(weights_ref, trig_ref, legendre_ref, rows, chosen):
    return (dot(weights_ref[rows, :], legendre_ref[...]) * dot(trig_ref[rows, :], chosen)).astype(BF16)


def first_kernel(weights_ref, trig_ref, code_ref, legendre_ref, design_ref):
    step = pl.program_id(0)
    chosen = one_hot(code_ref[...])
    for first in range(0, design_ref.shape[1], ROWS):
        rows = slice(first, first + ROWS)
        design_ref[step, rows, :] = design_tile(weights_ref, trig_ref, legendre_ref, rows, chosen)


def second_kernel(blocks, weights_ref, trig_ref, code_ref, legendre_ref, old_ref, *refs):
    probe_refs, old_probe_refs = refs[:blocks], refs[blocks : 2 * blocks]
    design_ref, pred_ref, sent_ref, total_ref = refs[2 * blocks :]
    step = pl.program_id(0)

    @pl.when(step == 0)
    def _():
        total_ref[...] = jnp.zeros_like(total_ref)

    probes = jnp.concatenate([ref[...] for ref in probe_refs], axis=0)
    old_probes = jnp.concatenate([ref[...] for ref in old_probe_refs], axis=0)
    chosen = one_hot(code_ref[...])
    for first in range(0, design_ref.shape[1], ROWS):
        rows = slice(first, first + ROWS)
        tile = design_tile(weights_ref, trig_ref, legendre_ref, rows, chosen)
        design_ref[step, rows, :] = tile
        total_ref[rows, :] += dot_t(tile, probes) + dot_t(old_ref[step, rows, :], old_probes)

    @pl.when(step == pl.num_programs(0) - 1)
    def _():
        total = jnp.transpose(total_ref[...])
        pred_ref[...] = total
        sent_ref[...] = total.astype(BF16)


def tables_kernel(seg_ref, bank_ref, high_ref, low_ref):
    for segment in range(high_ref.shape[0]):
        taps = bank_ref[pl.ds(seg_ref[segment], 1), :]
        spread = jnp.broadcast_to(taps, (2 * SEG, 2 * SEG))
        table = pltpu.roll(spread, SEG, 1, stride=1, stride_axis=0)[:, :SEG]
        high = table.astype(BF16)
        high_ref[segment] = high
        low_ref[segment] = (table - high.astype(F32)).astype(BF16)


def filter_kernel(bits, before_ref, pred_ref, high_ref, low_ref, out_ref):
    before = before_ref[...]
    count = before.shape[0]
    here = lax.axis_index("epoch")
    differing = here ^ (here - 1)
    place = lax.broadcasted_iota(jnp.int32, before.shape, 0)
    stride = count
    for bit in bits:
        stride //= 2
        up, down = pltpu.roll(before, stride, 0), pltpu.roll(before, count - stride, 0)
        flipped = jnp.where((place & stride) != 0, up, down)
        before = jnp.where((differing & bit) != 0, flipped, before)

    for segment in range(pred_ref.shape[1] // SEG):
        here = pred_ref[:, segment * SEG : (segment + 1) * SEG]
        past = before if segment == 0 else pred_ref[:, (segment - 1) * SEG : segment * SEG]
        window = jnp.concatenate([past, here], axis=1)
        high = window.astype(BF16)
        low = (window - high.astype(F32)).astype(BF16)
        value = dot(high, high_ref[segment]) + (dot(high, low_ref[segment]) + dot(low, high_ref[segment]))
        out_ref[:, segment * SEG : (segment + 1) * SEG] = value.astype(BF16)


def residual_kernel(filtered_ref, design_ref, kept_ref, sent_ref):
    value = dot(filtered_ref[...], design_ref[pl.program_id(0)])
    half = kept_ref.shape[0]
    kept_ref[...] = value[:half]
    sent_ref[...] = value[half:].astype(BF16)


def struct(shape, dtype):
    return jax.ShapeDtypeStruct(shape, dtype)


def whole(shape):
    return pl.BlockSpec(shape, lambda c: (0,) * len(shape))


def across(rows, cols, shift=0):
    return pl.BlockSpec((rows, cols), lambda c: (0, c + shift))


def in_hbm(array):
    return pltpu.with_memory_space_constraint(array, pltpu.HBM)


def resident(array):
    return pltpu.with_memory_space_constraint(array, pltpu.VMEM)


def cost(flops, nbytes):
    return pl.CostEstimate(flops=flops, bytes_accessed=nbytes, transcendentals=0)


def swapped(array, axis, bit):
    size = lax.axis_size(axis)
    return lax.ppermute(array, axis, [(i, i ^ bit) for i in range(size)])


def bits_of(axis):
    return [1 << b for b in range(lax.axis_size(axis).bit_length() - 1)]


def local(probes, lat_bin, lat_frac, longitude, order_code, legendre, bank, seg_filter):
    epochs, (nodes, coeffs) = lat_bin.shape[0], legendre.shape
    own = probes.shape[0]
    epoch_bits = bits_of("epoch")
    row = lambda array: array.reshape(1, -1)
    codes = row(order_code)
    legendre, codes = in_hbm(legendre), in_hbm(codes)
    half = coeffs // 2
    cols = min(COLS, half)
    steps = half // cols

    vmem, smem = pl.BlockSpec(memory_space=pltpu.VMEM), pl.BlockSpec(memory_space=pltpu.SMEM)
    taps = jnp.pad(bank, ((0, 0), (0, 2 * SEG - bank.shape[1])))
    segments = epochs // SEG
    high, low = pl.pallas_call(
        tables_kernel,
        in_specs=[smem, vmem],
        out_specs=[vmem] * 2,
        out_shape=[struct((segments, 2 * SEG, SEG), BF16)] * 2,
        cost_estimate=cost(40 * segments * SEG * SEG, 8 * segments * SEG * SEG),
        compiler_params=pltpu.CompilerParams(vmem_limit_bytes=SMALL_VMEM),
        name="tables",
    )(seg_filter, taps)

    weights, trig = pl.pallas_call(
        trig_kernel,
        grid=(1,),
        in_specs=[whole((1, epochs))] * 3,
        out_specs=[vmem] * 2,
        out_shape=[
            pltpu.VMEM((epochs, nodes), BF16),
            pltpu.VMEM((epochs, 2 * ORDERS), BF16),
        ],
        cost_estimate=cost(40 * epochs * ORDERS, 12 * epochs),
        compiler_params=pltpu.CompilerParams(vmem_limit_bytes=SMALL_VMEM),
        name="trig",
    )(in_hbm(row(lat_bin)), in_hbm(row(lat_frac)), in_hbm(row(longitude)))
    probes, weights = lax.optimization_barrier((probes, weights))
    angular = [resident(weights), resident(trig)]

    blocks = [probes]
    for bit in reversed(epoch_bits[1:]):
        blocks += [swapped(block, "epoch", bit) for block in blocks]

    design_1 = pl.pallas_call(
        first_kernel,
        grid=(steps,),
        in_specs=[vmem] * 2 + [across(1, cols), across(nodes, cols)],
        out_specs=vmem,
        out_shape=pltpu.VMEM((steps, epochs, cols), BF16),
        cost_estimate=cost(2 * epochs * half * (nodes + 2 * ORDERS), 2 * half * nodes),
        compiler_params=pltpu.CompilerParams(vmem_limit_bytes=KERNEL_VMEM),
        name="design_first",
    )(*angular, codes, legendre)
    blocks, design_1 = lax.optimization_barrier((blocks, design_1))
    blocks = blocks + [swapped(block, "epoch", epoch_bits[0]) for block in blocks]
    count = own * len(blocks)
    if own % 16:
        blocks = [jnp.concatenate(blocks, axis=0)]
    height = blocks[0].shape[0]

    design_2, pred, sent = pl.pallas_call(
        functools.partial(second_kernel, len(blocks)),
        grid=(steps,),
        in_specs=[
            vmem,
            vmem,
            across(1, cols, steps),
            across(nodes, cols, steps),
            vmem,
        ]
        + [across(height, cols, steps)] * len(blocks)
        + [across(height, cols)] * len(blocks),
        out_specs=[vmem, whole((count, epochs)), whole((count, epochs))],
        out_shape=[
            pltpu.VMEM((steps, epochs, cols), BF16),
            struct((count, epochs), F32),
            struct((count, epochs), BF16),
        ],
        scratch_shapes=[pltpu.VMEM((epochs, count), F32)],
        cost_estimate=cost(2 * epochs * half * (nodes + 2 * ORDERS + 2 * count), 2 * half * (2 * epochs + nodes)),
        compiler_params=pltpu.CompilerParams(vmem_limit_bytes=KERNEL_VMEM),
        name="design_second",
    )(*angular, codes, legendre, resident(design_1), *blocks, *blocks)

    for bit in bits_of("param"):
        pred = pred + swapped(sent, "param", bit).astype(F32)
        sent = pred.astype(BF16)

    devices = lax.axis_size("epoch")
    before = lax.ppermute(pred[:, epochs - SEG :], "epoch", [(i, i + 1) for i in range(devices - 1)])
    filtered = pl.pallas_call(
        functools.partial(filter_kernel, epoch_bits),
        in_specs=[vmem] * 4,
        out_specs=vmem,
        out_shape=struct((count, epochs), BF16),
        cost_estimate=cost(6 * count * epochs * 2 * SEG, 8 * count * epochs),
        compiler_params=pltpu.CompilerParams(vmem_limit_bytes=SMALL_VMEM),
        name="filter",
    )(before, pred, high, low)

    pieces = []
    for design in (design_1, design_2):
        kept, sent = pl.pallas_call(
            residual_kernel,
            grid=(steps,),
            in_specs=[whole((count, epochs)), vmem],
            out_specs=[across(count // 2, cols)] * 2,
            out_shape=[struct((count // 2, half), F32), struct((count // 2, half), BF16)],
            cost_estimate=cost(2 * count * epochs * half, 6 * count * half),
            compiler_params=pltpu.CompilerParams(vmem_limit_bytes=SMALL_VMEM),
            name="residual",
        )(filtered, resident(design))
        for bit in epoch_bits[:-1]:
            total = kept + swapped(sent, "epoch", bit).astype(F32)
            rows = total.shape[0] // 2
            kept, sent = total[:rows], total[rows:].astype(BF16)
        filtered, sent = lax.optimization_barrier((filtered, sent))
        received = swapped(sent, "epoch", epoch_bits[-1])
        pieces.append(kept + received.astype(F32))
    return jnp.concatenate(pieces, axis=1)


def solution(mesh):
    placed = (
        P(("groups", "epoch"), "param"),
        P("epoch"),
        P("epoch"),
        P("epoch"),
        P("param"),
        P(None, "param"),
        P(),
        P("epoch"),
    )
    return jax.shard_map(
        local,
        mesh=mesh,
        in_specs=placed,
        out_specs=P(("groups", "epoch"), "param"),
        check_vma=False,
    )
```

```python
import functools

import jax
import jax.numpy as jnp
from jax import lax
from jax.experimental import pallas as pl
from jax.experimental.pallas import tpu as pltpu
from jax.sharding import PartitionSpec as P


SEG = 256
ORDERS = 256
ROWS = 256
COLS = 1024
LANES = 128
TILE = 256
FIRST_COMPUTED, SECOND_COMPUTED = (1,), (1, 3)
KERNEL_VMEM = 10 << 20
SMALL_VMEM = 6 << 20
INV_TWO_PI = 0.15915494309189535
TURN = 12582912.0
COS = (0.9999992251396179, -19.738981246948242, 64.92865753173828, -85.27162170410156, 58.79049301147461, -21.07110595703125)
SIN = (6.283185005187988, -41.341590881347656, 81.59994506835938, -76.61447143554688, 41.3428840637207, -12.471243858337402)
BF16 = jnp.bfloat16
F32 = jnp.float32


def horner(coefficients, x):
    total = coefficients[-1]
    for coefficient in coefficients[-2::-1]:
        total = total * x + coefficient
    return total


def dot(a, b):
    return jnp.dot(a, b, preferred_element_type=F32)


def dot_t(a, b):
    return lax.dot_general(a, b, (((1,), (1,)), ((), ())), preferred_element_type=F32)


def spread(row):
    return jnp.transpose(jnp.broadcast_to(row, (LANES, row.shape[1])))


def fraction_of(turns):
    return turns - ((turns + TURN) - TURN)


def trig_kernel(bin_ref, frac_ref, lon_ref, weights_ref, trig_ref, turns_ref):
    nodes = weights_ref.shape[1]
    lane = lax.broadcasted_iota(jnp.int32, (1, LANES), 1).astype(F32)
    for first in range(0, weights_ref.shape[0], LANES):
        rows = slice(first, first + LANES)
        bins, fraction = spread(bin_ref[:, rows].astype(F32)), spread(frac_ref[:, rows])
        lower, upper = 1.0 - fraction, fraction
        for at in range(0, nodes, LANES):
            distance = bins - (lane + at)
            value = jnp.where(distance == 0.0, lower, jnp.where(distance == -1.0, upper, 0.0))
            weights_ref[rows, at : at + LANES] = value.astype(BF16)
        turns_row = lon_ref[:, rows] * INV_TWO_PI
        turns = spread(turns_row)
        turns_ref[rows, :] = turns
        rest, far = fraction_of(turns * lane), fraction_of(turns_row * LANES)
        square, far_square = rest * rest, far * far
        cos, sin = horner(COS, square), rest * horner(SIN, square)
        far_cos, far_sin = spread(horner(COS, far_square)), spread(far * horner(SIN, far_square))
        for part in range(ORDERS // LANES):
            if part:
                cos, sin = cos * far_cos - sin * far_sin, sin * far_cos + cos * far_sin
            at = part * LANES
            trig_ref[rows, at : at + LANES] = cos.astype(BF16)
            trig_ref[rows, ORDERS + at : ORDERS + at + LANES] = sin.astype(BF16)


def one_hot(code):
    place = lax.shift_right_logical(code, 1) + (code & 1) * ORDERS
    index = lax.broadcasted_iota(jnp.int32, (2 * ORDERS, 1), 0)
    return jnp.where(index == place, 1.0, 0.0).astype(BF16)


def build_design(weights_ref, trig_ref, turns_ref, code_ref, legendre_ref, design_ref, phase_ref, step, computed, after):
    code = code_ref[...]
    cols = code.shape[1]
    order = lax.shift_right_logical(code, 1).astype(F32)
    offset = (code & 1).astype(F32) * -0.25
    tiles = [slice(at, at + TILE) for at in range(0, cols, TILE)]
    chosen = {}
    for n, tile in enumerate(tiles):
        if n not in computed:
            chosen[n] = one_hot(code[:, tile])

    def compute(first):
        rows = slice(first, first + ROWS)
        for place, n in enumerate(computed):
            for at in range(0, TILE, LANES):
                lanes = slice(tiles[n].start + at, tiles[n].start + at + LANES)
                rest = fraction_of(turns_ref[rows, :] * order[:, lanes] + offset[:, lanes])
                phase_ref[rows, place * TILE + at : place * TILE + at + LANES] = horner(COS, rest * rest)

    compute(0)
    for first in range(0, design_ref.shape[1], ROWS):
        rows = slice(first, first + ROWS)
        if first + ROWS < design_ref.shape[1]:
            compute(first + ROWS)
        for n, tile in enumerate(tiles):
            interp = dot(weights_ref[rows, :], legendre_ref[:, tile])
            if n in chosen:
                phase = dot(trig_ref[rows, :], chosen[n])
            else:
                place = computed.index(n) * TILE
                phase = phase_ref[rows, place : place + TILE]
            design_ref[step, rows, tile] = (interp * phase).astype(BF16)
        after(rows)


def first_kernel(weights_ref, trig_ref, turns_ref, code_ref, legendre_ref, design_ref, phase_ref):
    step = pl.program_id(0)
    build_design(weights_ref, trig_ref, turns_ref, code_ref, legendre_ref, design_ref, phase_ref, step, FIRST_COMPUTED, lambda rows: None)


def second_kernel(blocks, weights_ref, trig_ref, turns_ref, code_ref, legendre_ref, old_ref, *refs):
    probe_refs, old_probe_refs = refs[:blocks], refs[blocks : 2 * blocks]
    design_ref, pred_ref, sent_ref, total_ref, phase_ref = refs[2 * blocks :]
    step = pl.program_id(0)

    @pl.when(step == 0)
    def _():
        total_ref[...] = jnp.zeros_like(total_ref)

    probes = jnp.concatenate([ref[...] for ref in probe_refs], axis=0)
    old_probes = jnp.concatenate([ref[...] for ref in old_probe_refs], axis=0)

    def predict(rows):
        total_ref[rows, :] += dot_t(design_ref[step, rows, :], probes) + dot_t(old_ref[step, rows, :], old_probes)

    build_design(weights_ref, trig_ref, turns_ref, code_ref, legendre_ref, design_ref, phase_ref, step, SECOND_COMPUTED, predict)

    @pl.when(step == pl.num_programs(0) - 1)
    def _():
        total = jnp.transpose(total_ref[...])
        pred_ref[...] = total
        sent_ref[...] = total.astype(BF16)


def tables_kernel(seg_ref, bank_ref, high_ref, low_ref):
    for segment in range(high_ref.shape[0]):
        taps = bank_ref[pl.ds(seg_ref[segment], 1), :]
        spread = jnp.broadcast_to(taps, (2 * SEG, 2 * SEG))
        table = pltpu.roll(spread, SEG, 1, stride=1, stride_axis=0)[:, :SEG]
        high = table.astype(BF16)
        high_ref[segment] = high
        low_ref[segment] = (table - high.astype(F32)).astype(BF16)


def filter_kernel(bits, before_ref, pred_ref, high_ref, low_ref, out_ref):
    before = before_ref[...]
    count = before.shape[0]
    here = lax.axis_index("epoch")
    differing = here ^ (here - 1)
    place = lax.broadcasted_iota(jnp.int32, before.shape, 0)
    stride = count
    for bit in bits:
        stride //= 2
        up, down = pltpu.roll(before, stride, 0), pltpu.roll(before, count - stride, 0)
        flipped = jnp.where((place & stride) != 0, up, down)
        before = jnp.where((differing & bit) != 0, flipped, before)

    for segment in range(pred_ref.shape[1] // SEG):
        here = pred_ref[:, segment * SEG : (segment + 1) * SEG]
        past = before if segment == 0 else pred_ref[:, (segment - 1) * SEG : segment * SEG]
        window = jnp.concatenate([past, here], axis=1)
        high = window.astype(BF16)
        low = (window - high.astype(F32)).astype(BF16)
        value = dot(high, high_ref[segment]) + (dot(high, low_ref[segment]) + dot(low, high_ref[segment]))
        out_ref[:, segment * SEG : (segment + 1) * SEG] = value.astype(BF16)


def residual_kernel(filtered_ref, design_ref, kept_ref, sent_ref):
    half, cols = kept_ref.shape[0], design_ref.shape[2]
    for step in range(design_ref.shape[0]):
        value = dot(filtered_ref[...], design_ref[step])
        kept_ref[:, step * cols : (step + 1) * cols] = value[:half]
        sent_ref[:, step * cols : (step + 1) * cols] = value[half:].astype(BF16)


def struct(shape, dtype):
    return jax.ShapeDtypeStruct(shape, dtype)


def whole(shape):
    return pl.BlockSpec(shape, lambda c: (0,) * len(shape))


def across(rows, cols, shift=0):
    return pl.BlockSpec((rows, cols), lambda c: (0, c + shift))


def in_hbm(array):
    return pltpu.with_memory_space_constraint(array, pltpu.HBM)


def resident(array):
    return pltpu.with_memory_space_constraint(array, pltpu.VMEM)


def cost(flops, nbytes):
    return pl.CostEstimate(flops=flops, bytes_accessed=nbytes, transcendentals=0)


def swapped(array, axis, bit):
    size = lax.axis_size(axis)
    return lax.ppermute(array, axis, [(i, i ^ bit) for i in range(size)])


def bits_of(axis):
    return [1 << b for b in range(lax.axis_size(axis).bit_length() - 1)]


def local(probes, lat_bin, lat_frac, longitude, order_code, legendre, bank, seg_filter):
    epochs, (nodes, coeffs) = lat_bin.shape[0], legendre.shape
    own = probes.shape[0]
    epoch_bits = bits_of("epoch")
    row = lambda array: array.reshape(1, -1)
    codes = row(order_code)
    legendre, codes = in_hbm(legendre), in_hbm(codes)
    half = coeffs // 2
    cols = min(COLS, half)
    steps = half // cols

    vmem, smem = pl.BlockSpec(memory_space=pltpu.VMEM), pl.BlockSpec(memory_space=pltpu.SMEM)
    taps = jnp.pad(bank, ((0, 0), (0, 2 * SEG - bank.shape[1])))
    segments = epochs // SEG
    high, low = pl.pallas_call(
        tables_kernel,
        in_specs=[smem, vmem],
        out_specs=[vmem] * 2,
        out_shape=[struct((segments, 2 * SEG, SEG), BF16)] * 2,
        cost_estimate=cost(40 * segments * SEG * SEG, 8 * segments * SEG * SEG),
        compiler_params=pltpu.CompilerParams(vmem_limit_bytes=SMALL_VMEM),
        name="tables",
    )(seg_filter, taps)

    weights, trig, turns = pl.pallas_call(
        trig_kernel,
        grid=(1,),
        in_specs=[whole((1, epochs))] * 3,
        out_specs=[vmem] * 3,
        out_shape=[
            pltpu.VMEM((epochs, nodes), BF16),
            pltpu.VMEM((epochs, 2 * ORDERS), BF16),
            pltpu.VMEM((epochs, LANES), F32),
        ],
        cost_estimate=cost(40 * epochs * ORDERS, 12 * epochs),
        compiler_params=pltpu.CompilerParams(vmem_limit_bytes=SMALL_VMEM),
        name="trig",
    )(in_hbm(row(lat_bin)), in_hbm(row(lat_frac)), in_hbm(row(longitude)))
    probes, weights = lax.optimization_barrier((probes, weights))
    angular = [resident(weights), resident(trig), resident(turns)]

    blocks = [probes]
    for bit in reversed(epoch_bits[1:]):
        blocks += [swapped(block, "epoch", bit) for block in blocks]

    design_1 = pl.pallas_call(
        first_kernel,
        grid=(steps,),
        in_specs=[vmem] * 3 + [across(1, cols), across(nodes, cols)],
        out_specs=vmem,
        out_shape=pltpu.VMEM((steps, epochs, cols), BF16),
        scratch_shapes=[pltpu.VMEM((epochs, TILE * len(FIRST_COMPUTED)), F32)],
        cost_estimate=cost(2 * epochs * half * (nodes + 2 * ORDERS), 2 * half * nodes),
        compiler_params=pltpu.CompilerParams(vmem_limit_bytes=KERNEL_VMEM),
        name="design_first",
    )(*angular, codes, legendre)
    blocks, design_1 = lax.optimization_barrier((blocks, design_1))
    blocks = blocks + [swapped(block, "epoch", epoch_bits[0]) for block in blocks]
    count = own * len(blocks)
    if own % 16:
        blocks = [jnp.concatenate(blocks, axis=0)]
    height = blocks[0].shape[0]

    design_2, pred, sent = pl.pallas_call(
        functools.partial(second_kernel, len(blocks)),
        grid=(steps,),
        in_specs=[
            vmem,
            vmem,
            vmem,
            across(1, cols, steps),
            across(nodes, cols, steps),
            vmem,
        ]
        + [across(height, cols, steps)] * len(blocks)
        + [across(height, cols)] * len(blocks),
        out_specs=[vmem, whole((count, epochs)), whole((count, epochs))],
        out_shape=[
            pltpu.VMEM((steps, epochs, cols), BF16),
            struct((count, epochs), F32),
            struct((count, epochs), BF16),
        ],
        scratch_shapes=[pltpu.VMEM((epochs, count), F32), pltpu.VMEM((epochs, TILE * len(SECOND_COMPUTED)), F32)],
        cost_estimate=cost(2 * epochs * half * (nodes + 2 * ORDERS + 2 * count), 2 * half * (2 * epochs + nodes)),
        compiler_params=pltpu.CompilerParams(vmem_limit_bytes=KERNEL_VMEM),
        name="design_second",
    )(*angular, codes, legendre, resident(design_1), *blocks, *blocks)

    for bit in bits_of("param"):
        pred = pred + swapped(sent, "param", bit).astype(F32)
        sent = pred.astype(BF16)

    devices = lax.axis_size("epoch")
    before = lax.ppermute(pred[:, epochs - SEG :], "epoch", [(i, i + 1) for i in range(devices - 1)])
    filtered = pl.pallas_call(
        functools.partial(filter_kernel, epoch_bits),
        in_specs=[vmem] * 4,
        out_specs=vmem,
        out_shape=struct((count, epochs), BF16),
        cost_estimate=cost(6 * count * epochs * 2 * SEG, 8 * count * epochs),
        compiler_params=pltpu.CompilerParams(vmem_limit_bytes=SMALL_VMEM),
        name="filter",
    )(before, pred, high, low)

    pieces = []
    for design in (design_1, design_2):
        kept, sent = pl.pallas_call(
            residual_kernel,
            in_specs=[vmem] * 2,
            out_specs=[vmem] * 2,
            out_shape=[pltpu.VMEM((count // 2, half), F32), pltpu.VMEM((count // 2, half), BF16)],
            cost_estimate=cost(2 * count * epochs * half, 6 * count * half),
            compiler_params=pltpu.CompilerParams(vmem_limit_bytes=SMALL_VMEM),
            name="residual",
        )(filtered, resident(design))
        for bit in epoch_bits[:-1]:
            total = kept + swapped(sent, "epoch", bit).astype(F32)
            rows = total.shape[0] // 2
            kept, sent = total[:rows], total[rows:].astype(BF16)
        filtered, sent = lax.optimization_barrier((filtered, sent))
        received = swapped(sent, "epoch", epoch_bits[-1])
        pieces.append(kept + received.astype(F32))
    return jnp.concatenate(pieces, axis=1)


def solution(mesh):
    placed = (
        P(("groups", "epoch"), "param"),
        P("epoch"),
        P("epoch"),
        P("epoch"),
        P("param"),
        P(None, "param"),
        P(),
        P("epoch"),
    )
    return jax.shard_map(
        local,
        mesh=mesh,
        in_specs=placed,
        out_specs=P(("groups", "epoch"), "param"),
        check_vma=False,
    )
```

```python
import functools

import jax
import jax.numpy as jnp
from jax import lax
from jax.experimental import pallas as pl
from jax.experimental.pallas import tpu as pltpu
from jax.sharding import PartitionSpec as P


SEG = 256
ORDERS = 256
ROWS = 256
COLS = 1024
LANES = 128
TILE = 256
FIRST_COMPUTED, SECOND_COMPUTED = (2,), (1, 3)
KERNEL_VMEM = 10 << 20
SMALL_VMEM = 6 << 20
INV_TWO_PI = 0.15915494309189535
TURN = 12582912.0
COS = (0.9999992251396179, -19.738981246948242, 64.92865753173828, -85.27162170410156, 58.79049301147461, -21.07110595703125)
SIN = (6.283185005187988, -41.341590881347656, 81.59994506835938, -76.61447143554688, 41.3428840637207, -12.471243858337402)
BF16 = jnp.bfloat16
F32 = jnp.float32


def horner(coefficients, x):
    total = coefficients[-1]
    for coefficient in coefficients[-2::-1]:
        total = total * x + coefficient
    return total


def dot(a, b):
    return jnp.dot(a, b, preferred_element_type=F32)


def dot_t(a, b):
    return lax.dot_general(a, b, (((1,), (1,)), ((), ())), preferred_element_type=F32)


def spread(row):
    return jnp.transpose(jnp.broadcast_to(row, (LANES, row.shape[1])))


def fraction_of(turns):
    return turns - ((turns + TURN) - TURN)


def trig_kernel(bin_ref, frac_ref, lon_ref, weights_ref, trig_ref, turns_ref):
    nodes = weights_ref.shape[1]
    lane = lax.broadcasted_iota(jnp.int32, (1, LANES), 1).astype(F32)
    for first in range(0, weights_ref.shape[0], LANES):
        rows = slice(first, first + LANES)
        bins, fraction = spread(bin_ref[:, rows].astype(F32)), spread(frac_ref[:, rows])
        lower, upper = 1.0 - fraction, fraction
        for at in range(0, nodes, LANES):
            distance = bins - (lane + at)
            value = jnp.where(distance == 0.0, lower, jnp.where(distance == -1.0, upper, 0.0))
            weights_ref[rows, at : at + LANES] = value.astype(BF16)
        turns_row = lon_ref[:, rows] * INV_TWO_PI
        turns = spread(turns_row)
        turns_ref[rows, :] = turns
        rest, far = fraction_of(turns * lane), fraction_of(turns_row * LANES)
        square, far_square = rest * rest, far * far
        cos, sin = horner(COS, square), rest * horner(SIN, square)
        far_cos, far_sin = spread(horner(COS, far_square)), spread(far * horner(SIN, far_square))
        for part in range(ORDERS // LANES):
            if part:
                cos, sin = cos * far_cos - sin * far_sin, sin * far_cos + cos * far_sin
            at = part * LANES
            trig_ref[rows, at : at + LANES] = cos.astype(BF16)
            trig_ref[rows, ORDERS + at : ORDERS + at + LANES] = sin.astype(BF16)


def one_hot(code):
    place = lax.shift_right_logical(code, 1) + (code & 1) * ORDERS
    index = lax.broadcasted_iota(jnp.int32, (2 * ORDERS, 1), 0)
    return jnp.where(index == place, 1.0, 0.0).astype(BF16)


def build_design(weights_ref, trig_ref, turns_ref, code_ref, legendre_ref, design_ref, phase_ref, step, computed, after):
    code = code_ref[...]
    cols = code.shape[1]
    order = lax.shift_right_logical(code, 1).astype(F32)
    offset = (code & 1).astype(F32) * -0.25
    tiles = [slice(at, at + TILE) for at in range(0, cols, TILE)]
    chosen = {}
    for n, tile in enumerate(tiles):
        if n not in computed:
            chosen[n] = one_hot(code[:, tile])

    def compute(first):
        rows = slice(first, first + ROWS)
        for place, n in enumerate(computed):
            for at in range(0, TILE, LANES):
                lanes = slice(tiles[n].start + at, tiles[n].start + at + LANES)
                rest = fraction_of(turns_ref[rows, :] * order[:, lanes] + offset[:, lanes])
                phase_ref[rows, place * TILE + at : place * TILE + at + LANES] = horner(COS, rest * rest)

    compute(0)
    for first in range(0, design_ref.shape[1], ROWS):
        rows = slice(first, first + ROWS)
        if first + ROWS < design_ref.shape[1]:
            compute(first + ROWS)
        for n, tile in enumerate(tiles):
            interp = dot(weights_ref[rows, :], legendre_ref[:, tile])
            if n in chosen:
                phase = dot(trig_ref[rows, :], chosen[n])
            else:
                place = computed.index(n) * TILE
                phase = phase_ref[rows, place : place + TILE]
            design_ref[step, rows, tile] = (interp * phase).astype(BF16)
        after(rows)


def first_kernel(weights_ref, trig_ref, turns_ref, code_ref, legendre_ref, design_ref, phase_ref):
    step = pl.program_id(0)
    build_design(weights_ref, trig_ref, turns_ref, code_ref, legendre_ref, design_ref, phase_ref, step, FIRST_COMPUTED, lambda rows: None)


def second_kernel(blocks, weights_ref, trig_ref, turns_ref, code_ref, legendre_ref, old_ref, *refs):
    probe_refs, old_probe_refs = refs[:blocks], refs[blocks : 2 * blocks]
    design_ref, pred_ref, sent_ref, total_ref, phase_ref = refs[2 * blocks :]
    step = pl.program_id(0)

    @pl.when(step == 0)
    def _():
        total_ref[...] = jnp.zeros_like(total_ref)

    probes = jnp.concatenate([ref[...] for ref in probe_refs], axis=0)
    old_probes = jnp.concatenate([ref[...] for ref in old_probe_refs], axis=0)

    def predict(rows):
        total_ref[rows, :] += dot_t(design_ref[step, rows, :], probes) + dot_t(old_ref[step, rows, :], old_probes)

    build_design(weights_ref, trig_ref, turns_ref, code_ref, legendre_ref, design_ref, phase_ref, step, SECOND_COMPUTED, predict)

    @pl.when(step == pl.num_programs(0) - 1)
    def _():
        total = jnp.transpose(total_ref[...])
        pred_ref[...] = total
        sent_ref[...] = total.astype(BF16)


def tables_kernel(seg_ref, bank_ref, high_ref, low_ref):
    for segment in range(high_ref.shape[0]):
        taps = bank_ref[pl.ds(seg_ref[segment], 1), :]
        spread = jnp.broadcast_to(taps, (2 * SEG, 2 * SEG))
        table = pltpu.roll(spread, SEG, 1, stride=1, stride_axis=0)[:, :SEG]
        high = table.astype(BF16)
        high_ref[segment] = high
        low_ref[segment] = (table - high.astype(F32)).astype(BF16)


def filter_kernel(bits, before_ref, pred_ref, high_ref, low_ref, out_ref):
    before = before_ref[...]
    count = before.shape[0]
    here = lax.axis_index("epoch")
    differing = here ^ (here - 1)
    place = lax.broadcasted_iota(jnp.int32, before.shape, 0)
    stride = count
    for bit in bits:
        stride //= 2
        up, down = pltpu.roll(before, stride, 0), pltpu.roll(before, count - stride, 0)
        flipped = jnp.where((place & stride) != 0, up, down)
        before = jnp.where((differing & bit) != 0, flipped, before)

    for segment in range(pred_ref.shape[1] // SEG):
        here = pred_ref[:, segment * SEG : (segment + 1) * SEG]
        past = before if segment == 0 else pred_ref[:, (segment - 1) * SEG : segment * SEG]
        window = jnp.concatenate([past, here], axis=1)
        high = window.astype(BF16)
        low = (window - high.astype(F32)).astype(BF16)
        value = dot(high, high_ref[segment]) + (dot(high, low_ref[segment]) + dot(low, high_ref[segment]))
        out_ref[:, segment * SEG : (segment + 1) * SEG] = value.astype(BF16)


def residual_kernel(filtered_ref, design_ref, kept_ref, sent_ref):
    half, cols = kept_ref.shape[0], design_ref.shape[2]
    for step in range(design_ref.shape[0]):
        value = dot(filtered_ref[...], design_ref[step])
        kept_ref[:, step * cols : (step + 1) * cols] = value[:half]
        sent_ref[:, step * cols : (step + 1) * cols] = value[half:].astype(BF16)


def struct(shape, dtype):
    return jax.ShapeDtypeStruct(shape, dtype)


def whole(shape):
    return pl.BlockSpec(shape, lambda c: (0,) * len(shape))


def across(rows, cols, shift=0):
    return pl.BlockSpec((rows, cols), lambda c: (0, c + shift))


def in_hbm(array):
    return pltpu.with_memory_space_constraint(array, pltpu.HBM)


def resident(array):
    return pltpu.with_memory_space_constraint(array, pltpu.VMEM)


def cost(flops, nbytes):
    return pl.CostEstimate(flops=flops, bytes_accessed=nbytes, transcendentals=0)


def swapped(array, axis, bit):
    size = lax.axis_size(axis)
    return lax.ppermute(array, axis, [(i, i ^ bit) for i in range(size)])


def bits_of(axis):
    return [1 << b for b in range(lax.axis_size(axis).bit_length() - 1)]


def local(probes, lat_bin, lat_frac, longitude, order_code, legendre, bank, seg_filter):
    epochs, (nodes, coeffs) = lat_bin.shape[0], legendre.shape
    own = probes.shape[0]
    epoch_bits = bits_of("epoch")
    row = lambda array: array.reshape(1, -1)
    codes = row(order_code)
    legendre, codes = in_hbm(legendre), in_hbm(codes)
    half = coeffs // 2
    cols = min(COLS, half)
    steps = half // cols

    vmem, smem = pl.BlockSpec(memory_space=pltpu.VMEM), pl.BlockSpec(memory_space=pltpu.SMEM)
    taps = jnp.pad(bank, ((0, 0), (0, 2 * SEG - bank.shape[1])))
    segments = epochs // SEG
    high, low = pl.pallas_call(
        tables_kernel,
        in_specs=[smem, vmem],
        out_specs=[vmem] * 2,
        out_shape=[struct((segments, 2 * SEG, SEG), BF16)] * 2,
        cost_estimate=cost(40 * segments * SEG * SEG, 8 * segments * SEG * SEG),
        compiler_params=pltpu.CompilerParams(vmem_limit_bytes=SMALL_VMEM),
        name="tables",
    )(seg_filter, taps)

    weights, trig, turns = pl.pallas_call(
        trig_kernel,
        grid=(1,),
        in_specs=[whole((1, epochs))] * 3,
        out_specs=[vmem] * 3,
        out_shape=[
            pltpu.VMEM((epochs, nodes), BF16),
            pltpu.VMEM((epochs, 2 * ORDERS), BF16),
            pltpu.VMEM((epochs, LANES), F32),
        ],
        cost_estimate=cost(40 * epochs * ORDERS, 12 * epochs),
        compiler_params=pltpu.CompilerParams(vmem_limit_bytes=SMALL_VMEM),
        name="trig",
    )(in_hbm(row(lat_bin)), in_hbm(row(lat_frac)), in_hbm(row(longitude)))
    probes, weights = lax.optimization_barrier((probes, weights))
    angular = [resident(weights), resident(trig), resident(turns)]

    blocks = [probes]
    for bit in reversed(epoch_bits[1:]):
        blocks += [swapped(block, "epoch", bit) for block in blocks]

    design_1 = pl.pallas_call(
        first_kernel,
        grid=(steps,),
        in_specs=[vmem] * 3 + [across(1, cols), across(nodes, cols)],
        out_specs=vmem,
        out_shape=pltpu.VMEM((steps, epochs, cols), BF16),
        scratch_shapes=[pltpu.VMEM((epochs, TILE * len(FIRST_COMPUTED)), F32)],
        cost_estimate=cost(2 * epochs * half * (nodes + 2 * ORDERS), 2 * half * nodes),
        compiler_params=pltpu.CompilerParams(vmem_limit_bytes=KERNEL_VMEM),
        name="design_first",
    )(*angular, codes, legendre)
    blocks, design_1 = lax.optimization_barrier((blocks, design_1))
    blocks = blocks + [swapped(block, "epoch", epoch_bits[0]) for block in blocks]
    count = own * len(blocks)
    if own % 16:
        blocks = [jnp.concatenate(blocks, axis=0)]
    height = blocks[0].shape[0]

    design_2, pred, sent = pl.pallas_call(
        functools.partial(second_kernel, len(blocks)),
        grid=(steps,),
        in_specs=[
            vmem,
            vmem,
            vmem,
            across(1, cols, steps),
            across(nodes, cols, steps),
            vmem,
        ]
        + [across(height, cols, steps)] * len(blocks)
        + [across(height, cols)] * len(blocks),
        out_specs=[vmem, whole((count, epochs)), whole((count, epochs))],
        out_shape=[
            pltpu.VMEM((steps, epochs, cols), BF16),
            struct((count, epochs), F32),
            struct((count, epochs), BF16),
        ],
        scratch_shapes=[pltpu.VMEM((epochs, count), F32), pltpu.VMEM((epochs, TILE * len(SECOND_COMPUTED)), F32)],
        cost_estimate=cost(2 * epochs * half * (nodes + 2 * ORDERS + 2 * count), 2 * half * (2 * epochs + nodes)),
        compiler_params=pltpu.CompilerParams(vmem_limit_bytes=KERNEL_VMEM),
        name="design_second",
    )(*angular, codes, legendre, resident(design_1), *blocks, *blocks)

    for bit in bits_of("param"):
        pred = pred + swapped(sent, "param", bit).astype(F32)
        sent = pred.astype(BF16)

    devices = lax.axis_size("epoch")
    before = lax.ppermute(pred[:, epochs - SEG :], "epoch", [(i, i + 1) for i in range(devices - 1)])
    filtered = pl.pallas_call(
        functools.partial(filter_kernel, epoch_bits),
        in_specs=[vmem] * 4,
        out_specs=vmem,
        out_shape=struct((count, epochs), BF16),
        cost_estimate=cost(6 * count * epochs * 2 * SEG, 8 * count * epochs),
        compiler_params=pltpu.CompilerParams(vmem_limit_bytes=SMALL_VMEM),
        name="filter",
    )(before, pred, high, low)

    pieces = []
    for design in (design_1, design_2):
        kept, sent = pl.pallas_call(
            residual_kernel,
            in_specs=[vmem] * 2,
            out_specs=[vmem] * 2,
            out_shape=[pltpu.VMEM((count // 2, half), F32), pltpu.VMEM((count // 2, half), BF16)],
            cost_estimate=cost(2 * count * epochs * half, 6 * count * half),
            compiler_params=pltpu.CompilerParams(vmem_limit_bytes=SMALL_VMEM),
            name="residual",
        )(filtered, resident(design))
        for bit in epoch_bits[:-1]:
            total = kept + swapped(sent, "epoch", bit).astype(F32)
            rows = total.shape[0] // 2
            kept, sent = total[:rows], total[rows:].astype(BF16)
        filtered, sent = lax.optimization_barrier((filtered, sent))
        received = swapped(sent, "epoch", epoch_bits[-1])
        pieces.append(kept + received.astype(F32))
    first, second = pieces
    result = lax.pad(first, jnp.zeros((), F32), ((0, 0, 0), (0, coeffs - half, 0)))
    return lax.dynamic_update_slice(result, second, (0, half))


def solution(mesh):
    placed = (
        P(("groups", "epoch"), "param"),
        P("epoch"),
        P("epoch"),
        P("epoch"),
        P("param"),
        P(None, "param"),
        P(),
        P("epoch"),
    )
    return jax.shard_map(
        local,
        mesh=mesh,
        in_specs=placed,
        out_specs=P(("groups", "epoch"), "param"),
        check_vma=False,
    )
```

```python
import functools

import jax
import jax.numpy as jnp
from jax import lax
from jax.experimental import pallas as pl
from jax.experimental.pallas import tpu as pltpu
from jax.sharding import PartitionSpec as P


SEG = 256
ORDERS = 256
ROWS = 256
COLS = 1024
LANES = 128
TILE = 256
FIRST_COMPUTED, SECOND_COMPUTED = (2,), (0, 3)
KERNEL_VMEM = 10 << 20
SMALL_VMEM = 6 << 20
INV_TWO_PI = 0.15915494309189535
TURN = 12582912.0
COS = (0.9999992251396179, -19.738981246948242, 64.92865753173828, -85.27162170410156, 58.79049301147461, -21.07110595703125)
SIN = (6.283185005187988, -41.341590881347656, 81.59994506835938, -76.61447143554688, 41.3428840637207, -12.471243858337402)
BF16 = jnp.bfloat16
F32 = jnp.float32


def horner(coefficients, x):
    total = coefficients[-1]
    for coefficient in coefficients[-2::-1]:
        total = total * x + coefficient
    return total


def dot(a, b):
    return jnp.dot(a, b, preferred_element_type=F32)


def dot_t(a, b):
    return lax.dot_general(a, b, (((1,), (1,)), ((), ())), preferred_element_type=F32)


def spread(row):
    return jnp.transpose(jnp.broadcast_to(row, (LANES, row.shape[1])))


def fraction_of(turns):
    return turns - ((turns + TURN) - TURN)


def trig_kernel(bin_ref, frac_ref, lon_ref, weights_ref, trig_ref, turns_ref):
    nodes = weights_ref.shape[1]
    lane = lax.broadcasted_iota(jnp.int32, (1, LANES), 1).astype(F32)
    for first in range(0, weights_ref.shape[0], LANES):
        rows = slice(first, first + LANES)
        bins, fraction = spread(bin_ref[:, rows].astype(F32)), spread(frac_ref[:, rows])
        lower, upper = 1.0 - fraction, fraction
        for at in range(0, nodes, LANES):
            distance = bins - (lane + at)
            value = jnp.where(distance == 0.0, lower, jnp.where(distance == -1.0, upper, 0.0))
            weights_ref[rows, at : at + LANES] = value.astype(BF16)
        turns_row = lon_ref[:, rows] * INV_TWO_PI
        turns = spread(turns_row)
        turns_ref[rows, :] = turns
        rest, far = fraction_of(turns * lane), fraction_of(turns_row * LANES)
        square, far_square = rest * rest, far * far
        cos, sin = horner(COS, square), rest * horner(SIN, square)
        far_cos, far_sin = spread(horner(COS, far_square)), spread(far * horner(SIN, far_square))
        for part in range(ORDERS // LANES):
            if part:
                cos, sin = cos * far_cos - sin * far_sin, sin * far_cos + cos * far_sin
            at = part * LANES
            trig_ref[rows, at : at + LANES] = cos.astype(BF16)
            trig_ref[rows, ORDERS + at : ORDERS + at + LANES] = sin.astype(BF16)


def one_hot(code):
    place = lax.shift_right_logical(code, 1) + (code & 1) * ORDERS
    index = lax.broadcasted_iota(jnp.int32, (2 * ORDERS, 1), 0)
    return jnp.where(index == place, 1.0, 0.0).astype(BF16)


def build_design(weights_ref, trig_ref, turns_ref, code_ref, legendre_ref, design_ref, phase_ref, step, computed, after):
    code = code_ref[...]
    cols = code.shape[1]
    order = lax.shift_right_logical(code, 1).astype(F32)
    offset = (code & 1).astype(F32) * -0.25
    tiles = [slice(at, at + TILE) for at in range(0, cols, TILE)]
    chosen = {}
    for n, tile in enumerate(tiles):
        if n not in computed:
            chosen[n] = one_hot(code[:, tile])

    def compute(first):
        rows = slice(first, first + ROWS)
        for place, n in enumerate(computed):
            for at in range(0, TILE, LANES):
                lanes = slice(tiles[n].start + at, tiles[n].start + at + LANES)
                rest = fraction_of(turns_ref[rows, :] * order[:, lanes] + offset[:, lanes])
                phase_ref[rows, place * TILE + at : place * TILE + at + LANES] = horner(COS, rest * rest)

    compute(0)
    for first in range(0, design_ref.shape[1], ROWS):
        rows = slice(first, first + ROWS)
        if first + ROWS < design_ref.shape[1]:
            compute(first + ROWS)
        for n, tile in enumerate(tiles):
            interp = dot(weights_ref[rows, :], legendre_ref[:, tile])
            if n in chosen:
                phase = dot(trig_ref[rows, :], chosen[n])
            else:
                place = computed.index(n) * TILE
                phase = phase_ref[rows, place : place + TILE]
            design_ref[step, rows, tile] = (interp * phase).astype(BF16)
        after(rows)


def first_kernel(weights_ref, trig_ref, turns_ref, code_ref, legendre_ref, design_ref, phase_ref):
    step = pl.program_id(0)
    build_design(weights_ref, trig_ref, turns_ref, code_ref, legendre_ref, design_ref, phase_ref, step, FIRST_COMPUTED, lambda rows: None)


def second_kernel(blocks, weights_ref, trig_ref, turns_ref, code_ref, legendre_ref, old_ref, *refs):
    probe_refs, old_probe_refs = refs[:blocks], refs[blocks : 2 * blocks]
    design_ref, pred_ref, sent_ref, total_ref, phase_ref = refs[2 * blocks :]
    step = pl.program_id(0)

    @pl.when(step == 0)
    def _():
        total_ref[...] = jnp.zeros_like(total_ref)

    probes = jnp.concatenate([ref[...] for ref in probe_refs], axis=0)
    old_probes = jnp.concatenate([ref[...] for ref in old_probe_refs], axis=0)

    def predict(rows):
        total_ref[rows, :] += dot_t(design_ref[step, rows, :], probes) + dot_t(old_ref[step, rows, :], old_probes)

    build_design(weights_ref, trig_ref, turns_ref, code_ref, legendre_ref, design_ref, phase_ref, step, SECOND_COMPUTED, predict)

    @pl.when(step == pl.num_programs(0) - 1)
    def _():
        total = jnp.transpose(total_ref[...])
        pred_ref[...] = total
        sent_ref[...] = total.astype(BF16)


def tables_kernel(seg_ref, bank_ref, high_ref, low_ref):
    for segment in range(high_ref.shape[0]):
        taps = bank_ref[pl.ds(seg_ref[segment], 1), :]
        spread = jnp.broadcast_to(taps, (2 * SEG, 2 * SEG))
        table = pltpu.roll(spread, SEG, 1, stride=1, stride_axis=0)[:, :SEG]
        high = table.astype(BF16)
        high_ref[segment] = high
        low_ref[segment] = (table - high.astype(F32)).astype(BF16)


def filter_kernel(bits, before_ref, pred_ref, high_ref, low_ref, out_ref):
    before = before_ref[...]
    count = before.shape[0]
    here = lax.axis_index("epoch")
    differing = here ^ (here - 1)
    place = lax.broadcasted_iota(jnp.int32, before.shape, 0)
    stride = count
    for bit in bits:
        stride //= 2
        up, down = pltpu.roll(before, stride, 0), pltpu.roll(before, count - stride, 0)
        flipped = jnp.where((place & stride) != 0, up, down)
        before = jnp.where((differing & bit) != 0, flipped, before)

    for segment in range(pred_ref.shape[1] // SEG):
        here = pred_ref[:, segment * SEG : (segment + 1) * SEG]
        past = before if segment == 0 else pred_ref[:, (segment - 1) * SEG : segment * SEG]
        window = jnp.concatenate([past, here], axis=1)
        high = window.astype(BF16)
        low = (window - high.astype(F32)).astype(BF16)
        value = dot(high, high_ref[segment]) + (dot(high, low_ref[segment]) + dot(low, high_ref[segment]))
        out_ref[:, segment * SEG : (segment + 1) * SEG] = value.astype(BF16)


def residual_kernel(filtered_ref, design_ref, kept_ref, sent_ref):
    half, cols = kept_ref.shape[0], design_ref.shape[2]
    for step in range(design_ref.shape[0]):
        value = dot(filtered_ref[...], design_ref[step])
        kept_ref[:, step * cols : (step + 1) * cols] = value[:half]
        sent_ref[:, step * cols : (step + 1) * cols] = value[half:].astype(BF16)


def struct(shape, dtype):
    return jax.ShapeDtypeStruct(shape, dtype)


def whole(shape):
    return pl.BlockSpec(shape, lambda c: (0,) * len(shape))


def across(rows, cols, shift=0):
    return pl.BlockSpec((rows, cols), lambda c: (0, c + shift))


def in_hbm(array):
    return pltpu.with_memory_space_constraint(array, pltpu.HBM)


def resident(array):
    return pltpu.with_memory_space_constraint(array, pltpu.VMEM)


def cost(flops, nbytes):
    return pl.CostEstimate(flops=flops, bytes_accessed=nbytes, transcendentals=0)


def swapped(array, axis, bit):
    size = lax.axis_size(axis)
    return lax.ppermute(array, axis, [(i, i ^ bit) for i in range(size)])


def bits_of(axis):
    return [1 << b for b in range(lax.axis_size(axis).bit_length() - 1)]


def local(probes, lat_bin, lat_frac, longitude, order_code, legendre, bank, seg_filter):
    epochs, (nodes, coeffs) = lat_bin.shape[0], legendre.shape
    own = probes.shape[0]
    epoch_bits = bits_of("epoch")
    row = lambda array: array.reshape(1, -1)
    codes = row(order_code)
    legendre, codes = in_hbm(legendre), in_hbm(codes)
    half = coeffs // 2
    cols = min(COLS, half)
    steps = half // cols

    vmem, smem = pl.BlockSpec(memory_space=pltpu.VMEM), pl.BlockSpec(memory_space=pltpu.SMEM)
    taps = jnp.pad(bank, ((0, 0), (0, 2 * SEG - bank.shape[1])))
    segments = epochs // SEG
    high, low = pl.pallas_call(
        tables_kernel,
        in_specs=[smem, vmem],
        out_specs=[vmem] * 2,
        out_shape=[struct((segments, 2 * SEG, SEG), BF16)] * 2,
        cost_estimate=cost(40 * segments * SEG * SEG, 8 * segments * SEG * SEG),
        compiler_params=pltpu.CompilerParams(vmem_limit_bytes=SMALL_VMEM),
        name="tables",
    )(seg_filter, taps)

    weights, trig, turns = pl.pallas_call(
        trig_kernel,
        grid=(1,),
        in_specs=[whole((1, epochs))] * 3,
        out_specs=[vmem] * 3,
        out_shape=[
            pltpu.VMEM((epochs, nodes), BF16),
            pltpu.VMEM((epochs, 2 * ORDERS), BF16),
            pltpu.VMEM((epochs, LANES), F32),
        ],
        cost_estimate=cost(40 * epochs * ORDERS, 12 * epochs),
        compiler_params=pltpu.CompilerParams(vmem_limit_bytes=SMALL_VMEM),
        name="trig",
    )(in_hbm(row(lat_bin)), in_hbm(row(lat_frac)), in_hbm(row(longitude)))
    probes, weights = lax.optimization_barrier((probes, weights))
    angular = [resident(weights), resident(trig), resident(turns)]

    blocks = [probes]
    for bit in reversed(epoch_bits[1:]):
        blocks += [swapped(block, "epoch", bit) for block in blocks]

    near = swapped(probes, "epoch", epoch_bits[0])
    design_1 = pl.pallas_call(
        first_kernel,
        grid=(steps,),
        in_specs=[vmem] * 3 + [across(1, cols), across(nodes, cols)],
        out_specs=vmem,
        out_shape=pltpu.VMEM((steps, epochs, cols), BF16),
        scratch_shapes=[pltpu.VMEM((epochs, TILE * len(FIRST_COMPUTED)), F32)],
        cost_estimate=cost(2 * epochs * half * (nodes + 2 * ORDERS), 2 * half * nodes),
        compiler_params=pltpu.CompilerParams(vmem_limit_bytes=KERNEL_VMEM),
        name="design_first",
    )(*angular, codes, legendre)
    far, design_1 = lax.optimization_barrier((blocks[1:], design_1))
    blocks = [probes, *far, near] + [swapped(block, "epoch", epoch_bits[0]) for block in far]
    count = own * len(blocks)
    if own % 16:
        blocks = [jnp.concatenate(blocks, axis=0)]
    height = blocks[0].shape[0]

    design_2, pred, sent = pl.pallas_call(
        functools.partial(second_kernel, len(blocks)),
        grid=(steps,),
        in_specs=[
            vmem,
            vmem,
            vmem,
            across(1, cols, steps),
            across(nodes, cols, steps),
            vmem,
        ]
        + [across(height, cols, steps)] * len(blocks)
        + [across(height, cols)] * len(blocks),
        out_specs=[vmem, whole((count, epochs)), whole((count, epochs))],
        out_shape=[
            pltpu.VMEM((steps, epochs, cols), BF16),
            struct((count, epochs), F32),
            struct((count, epochs), BF16),
        ],
        scratch_shapes=[pltpu.VMEM((epochs, count), F32), pltpu.VMEM((epochs, TILE * len(SECOND_COMPUTED)), F32)],
        cost_estimate=cost(2 * epochs * half * (nodes + 2 * ORDERS + 2 * count), 2 * half * (2 * epochs + nodes)),
        compiler_params=pltpu.CompilerParams(vmem_limit_bytes=KERNEL_VMEM),
        name="design_second",
    )(*angular, codes, legendre, resident(design_1), *blocks, *blocks)

    for bit in bits_of("param"):
        pred = pred + swapped(sent, "param", bit).astype(F32)
        sent = pred.astype(BF16)

    devices = lax.axis_size("epoch")
    before = lax.ppermute(pred[:, epochs - SEG :], "epoch", [(i, i + 1) for i in range(devices - 1)])
    filtered = pl.pallas_call(
        functools.partial(filter_kernel, epoch_bits),
        in_specs=[vmem] * 4,
        out_specs=vmem,
        out_shape=struct((count, epochs), BF16),
        cost_estimate=cost(6 * count * epochs * 2 * SEG, 8 * count * epochs),
        compiler_params=pltpu.CompilerParams(vmem_limit_bytes=SMALL_VMEM),
        name="filter",
    )(before, pred, high, low)

    pieces = []
    for design in (design_1, design_2):
        kept, sent = pl.pallas_call(
            residual_kernel,
            in_specs=[vmem] * 2,
            out_specs=[vmem] * 2,
            out_shape=[pltpu.VMEM((count // 2, half), F32), pltpu.VMEM((count // 2, half), BF16)],
            cost_estimate=cost(2 * count * epochs * half, 6 * count * half),
            compiler_params=pltpu.CompilerParams(vmem_limit_bytes=SMALL_VMEM),
            name="residual",
        )(filtered, resident(design))
        for bit in epoch_bits[:-1]:
            total = kept + swapped(sent, "epoch", bit).astype(F32)
            rows = total.shape[0] // 2
            kept, sent = total[:rows], total[rows:].astype(BF16)
        filtered, sent = lax.optimization_barrier((filtered, sent))
        received = swapped(sent, "epoch", epoch_bits[-1])
        pieces.append(kept + received.astype(F32))
    first, second = pieces
    result = lax.pad(first, jnp.zeros((), F32), ((0, 0, 0), (0, coeffs - half, 0)))
    return lax.dynamic_update_slice(result, second, (0, half))


def solution(mesh):
    placed = (
        P(("groups", "epoch"), "param"),
        P("epoch"),
        P("epoch"),
        P("epoch"),
        P("param"),
        P(None, "param"),
        P(),
        P("epoch"),
    )
    return jax.shard_map(
        local,
        mesh=mesh,
        in_specs=placed,
        out_specs=P(("groups", "epoch"), "param"),
        check_vma=False,
    )
```
